32 devices in a mesh: blk: 8 (over z, x), uly: 4 (over y, core).
Axes of the slice: x: 2, y: 2, z: 4, core: 2. Of those that a mesh axis runs over, the one named last changes fastest.
Arguments:
- query_projection: bfloat16 [4096, 4096], P(('blk', 'uly')), may hold values from -4.5 to 4.5
- key_projection: bfloat16 [4096, 512], P(('blk', 'uly')), may hold values from -4.5 to 4.5
- value_projection: bfloat16 [4096, 512], P(('blk', 'uly')), may hold values from -6 to 6
- doc_start: int32 [4096], P('blk'), may hold values from 0 to 4095, as said below
Outputs:
- attn: bfloat16 [4096, 4096], P(('blk', 'uly'))
The draws below stay inside these ranges and needn't reach their ends.
Inputs may be any that keep to these rules, and one draw needn't show every extreme that they name: Documents are contiguous runs of positions: doc_start[0] = 0, doc_start never falls, doc_start[i] <= i, and doc_start[doc_start[i]] = doc_start[i]. Every document has at most 1024 positions; the first has exactly 1024, and another of exactly 1024 begins strictly inside a block of 512 positions. The last position begins a document of its own.
All inputs are finite; a program needn't handle non-finite values.
Results may differ from the reference program's by a relative error of at most 0.0031.
Values may be sent and summed in bfloat16 or wider, within the bound.
A program may use at most 64 MiB of HBM per device.

```python
import jax
import jax.numpy as jnp
from jax import lax

QUERY_HEAD_COUNT = 32
KEY_VALUE_HEADS = 4
HEAD_WIDTH = 128
POSITION_GROUP = 512
BLOCK = 512
DOC_MAX = 1024
TOKEN_COUNT = 4096
N_BLK = 8


def drawn_pair(key):
    base = jax.random.fold_in(key, 7)
    key_query, key_random_keys = jax.random.split(base, 2)
    query_rows = jnp.clip(jax.random.normal(key_query, (TOKEN_COUNT, QUERY_HEAD_COUNT, HEAD_WIDTH), jnp.float32), -4.5, 4.5)
    key_rows = jnp.clip(jax.random.normal(key_random_keys, (TOKEN_COUNT, KEY_VALUE_HEADS, HEAD_WIDTH), jnp.float32), -4.5, 4.5)
    return (query_rows, key_rows)


def draw_query_projection(key, part):
    query_rows, key_rows = drawn_pair(key)
    return query_rows.reshape(TOKEN_COUNT, QUERY_HEAD_COUNT * HEAD_WIDTH).astype(jnp.bfloat16)


def draw_key_projection(key, part):
    query_rows, key_rows = drawn_pair(key)
    return key_rows.reshape(TOKEN_COUNT, KEY_VALUE_HEADS * HEAD_WIDTH).astype(jnp.bfloat16)


def draw_doc_start(key, part):
    base = jax.random.fold_in(key, 11)
    key_low, key_high, key_len, key_block, key_offset = jax.random.split(base, 5)
    top = DOC_MAX.bit_length() - 1
    expo = jnp.minimum(jax.random.randint(key_low, (TOKEN_COUNT,), 4, top + 1), jax.random.randint(key_high, (TOKEN_COUNT,), 4, top + 1))
    reach = jnp.left_shift(jnp.ones((TOKEN_COUNT,), jnp.int32), expo.astype(jnp.int32))
    lengths = jax.random.randint(key_len, (TOKEN_COUNT,), 1, reach + 1).astype(jnp.int32)
    lengths = lengths.at[0].set(DOC_MAX)
    ends = jnp.cumsum(lengths).astype(jnp.int32)
    starts = ends - lengths
    marks = jnp.zeros((TOKEN_COUNT,), jnp.int32).at[starts].set(1, mode='drop')
    marks = marks.at[0].set(1).at[TOKEN_COUNT - 1].set(1)
    token_places = jnp.arange(TOKEN_COUNT, dtype=jnp.int32)
    planted_block = jax.random.randint(key_block, (), 2, N_BLK - 2).astype(jnp.int32)
    planted = planted_block * BLOCK + jax.random.randint(key_offset, (), 1, BLOCK).astype(jnp.int32)
    inside = (token_places > planted) & (token_places < planted + DOC_MAX)
    marks = jnp.where(inside, 0, marks)
    marks = jnp.where((token_places == planted) | (token_places == planted + DOC_MAX), 1, marks)
    return lax.cummax(jnp.where(marks > 0, token_places, 0), axis=0).astype(jnp.int32)


def steps_of(stream_key, extent, pieces, least, top_value):
    def one(position, shards_of):
        heights = jax.random.uniform(jax.random.fold_in(jax.random.fold_in(stream_key, 6), position), (shards_of,), jnp.float32, least / len(pieces), top_value / len(pieces))
        return jnp.repeat(jnp.exp(heights), extent[position] // shards_of).reshape((-1,) + (1,) * (len(extent) - position - 1))

    factor_of = one(*pieces[0])
    for cut in pieces[1:]:
        factor_of = factor_of * one(*cut)
    return factor_of


def gaussian(own_key, shape, spread, most, shards=(), kind=jnp.bfloat16):
    drawn = spread * jax.random.normal(own_key, shape, jnp.float32)
    if shards:
        drawn = drawn * steps_of(own_key, shape, shards, -0.22, 0.18)
    return jnp.clip(drawn, -most, most).astype(kind)


def setup_inputs(seed: int = 0) -> dict:
    key_of = jax.random.split(jax.random.key(seed), 5)
    return {
        "query_projection": draw_query_projection(jax.random.fold_in(key_of[4], 71), 0),
        "key_projection": draw_key_projection(jax.random.fold_in(key_of[4], 71), 0),
        "value_projection": gaussian(key_of[2], (TOKEN_COUNT, KEY_VALUE_HEADS * HEAD_WIDTH), 1.0, 6.0, ((0, 32),)),
        "doc_start": draw_doc_start(jax.random.fold_in(key_of[4], 71), 0),
    }


def reference(query_projection, key_projection, value_projection, doc_start):
    token_rows = query_projection.shape[0]
    query_group_width = QUERY_HEAD_COUNT // KEY_VALUE_HEADS
    score_scale = HEAD_WIDTH ** -0.5
    query_rows = query_projection.reshape(token_rows, KEY_VALUE_HEADS, query_group_width, HEAD_WIDTH)
    key_rows = key_projection.reshape(token_rows, KEY_VALUE_HEADS, HEAD_WIDTH)
    value_rows = value_projection.reshape(token_rows, KEY_VALUE_HEADS, HEAD_WIDTH)

    def one_tile(index):
        start = index * POSITION_GROUP
        query_tile = lax.dynamic_slice_in_dim(query_rows, start, POSITION_GROUP, 0).astype(jnp.float32)
        starts = lax.dynamic_slice_in_dim(doc_start, start, POSITION_GROUP, 0)
        query_places = start + jnp.arange(POSITION_GROUP, dtype=jnp.int32)
        first_tile = (jnp.min(starts) // POSITION_GROUP).astype(jnp.int32)

        def add_tile(tile, carry):
            running_maximum, running_sum, running_output = carry
            key_start = tile * POSITION_GROUP
            key_tile = lax.dynamic_slice_in_dim(key_rows, key_start, POSITION_GROUP, 0).astype(jnp.float32)
            value_tile = lax.dynamic_slice_in_dim(value_rows, key_start, POSITION_GROUP, 0).astype(jnp.float32)
            key_places = key_start + jnp.arange(POSITION_GROUP, dtype=jnp.int32)
            seen = (key_places[None, :] >= starts[:, None]) & (key_places[None, :] <= query_places[:, None])
            seen = seen[:, None, None, :]
            scores = jnp.einsum("tkgd,nkd->tkgn", query_tile, key_tile) * score_scale
            masked = jnp.where(seen, scores, -1e30)
            fresh = jnp.maximum(running_maximum, jnp.max(masked, axis=-1))
            factor = jnp.exp(running_maximum - fresh)
            exps = jnp.where(seen, jnp.exp(masked - fresh[..., None]), 0.0)
            running_sum = running_sum * factor + jnp.sum(exps, axis=-1)
            rounded = exps.astype(jnp.bfloat16).astype(jnp.float32)
            running_output = running_output * factor[..., None] + jnp.einsum("tkgn,nkd->tkgd", rounded, value_tile)
            return fresh, running_sum, running_output

        running_maximum = jnp.full((POSITION_GROUP, KEY_VALUE_HEADS, query_group_width), -1e30, jnp.float32)
        running_sum = jnp.zeros((POSITION_GROUP, KEY_VALUE_HEADS, query_group_width), jnp.float32)
        running_output = jnp.zeros((POSITION_GROUP, KEY_VALUE_HEADS, query_group_width, HEAD_WIDTH), jnp.float32)
        running_maximum, running_sum, running_output = lax.fori_loop(first_tile, index + 1, add_tile, (running_maximum, running_sum, running_output))
        return (running_output / running_sum[..., None]).astype(jnp.bfloat16).reshape(POSITION_GROUP, QUERY_HEAD_COUNT * HEAD_WIDTH)

    outputs = lax.map(one_tile, jnp.arange(token_rows // POSITION_GROUP, dtype=jnp.int32))
    return outputs.reshape(token_rows, QUERY_HEAD_COUNT * HEAD_WIDTH)
```

```python
import functools

import jax
import jax.numpy as jnp
from jax import lax
from jax.experimental import pallas as pl
from jax.experimental.pallas import tpu as pltpu
from jax.sharding import PartitionSpec as P

HEAD_WIDTH = 128
LOOK_BACK_BLOCKS = 2
MASKED = -1e30
LOG2_E = 1.4426950408889634
MESH = pl.DeviceIdType.MESH


def each(count, looped, body, first=0):
    if looped:
        pl.loop(first, count)(body)
    else:
        for index in range(first, count):
            body(index)


def when(condition):
    if isinstance(condition, bool):
        return lambda body: body() if condition else None
    return pl.when(condition)


def kernel(
    blocks, width, heads, group, batch,
    q_hbm, k_hbm, v_hbm, start_ref, o_hbm,
    q_ref, k_win, v_win, bias, o_ref,
    local_sem, out_sem, shift_sem, lane_sem, pair_sem, recv_sem,
):
    tokens = q_hbm.shape[0]
    keys = (2 * width + 1) * tokens
    pairs = width // 2
    looped = pairs > 2
    b, u = lax.axis_index("blk"), lax.axis_index("uly")
    g, c = u // 2, u % 2
    sibling = g * 2 + (1 - c)
    has_1, has_2 = b >= 1, b >= 2
    hbm, win = (k_hbm, v_hbm), (k_win, v_win)

    def slot(which, h, index):
        start = pl.multiple_of(index * tokens, tokens)
        return win[which].at[h, pl.ds(start, tokens), :]

    def own(which, h):
        return hbm[which].at[:, lanes(h)]

    def lanes(index, count=1):
        span = count * HEAD_WIDTH
        return pl.ds(pl.multiple_of(index * span, span), span)

    def remote(src, h, which, index, send, device):
        return pltpu.make_async_remote_copy(
            src_ref=src,
            dst_ref=slot(which, h, index),
            send_sem=send,
            recv_sem=recv_sem.at[h, which, index],
            device_id=device,
            device_id_type=MESH,
        )

    def arrived(h, index):
        for which in range(2):
            ref = slot(which, h, index)
            remote(ref, h, which, index, shift_sem.at[h, which, 0], (b, sibling)).wait_recv()

    def shift_copies(h, act):
        for distance in range(1, LOOK_BACK_BLOCKS + 1):
            @pl.when(b + distance < blocks)
            def _():
                for which in range(2):
                    act(remote(own(which, h), h, which, (distance - 1) * width + u,
                               shift_sem.at[h, which, distance - 1], (b + distance, u)))

    def lane_own(h, act):
        @functools.partial(each, pairs, looped, first=1)
        def _(j):
            other = (g + j) % pairs
            @pl.when(other > g)
            def _():
                for which in range(2):
                    act(remote(own(which, h), h, which, width + u,
                               lane_sem.at[h, which, j - 1, 0], (b, other * 2 + c)))

    def pair_own(h, act):
        @pl.when(c == 0)
        def _():
            for which in range(2):
                act(remote(own(which, h), h, which, width + u,
                           pair_sem.at[h, which, 0, 0], (b, sibling)))

    def relay_1(h, act):
        @pl.when(has_1)
        def _():
            @functools.partial(each, pairs, looped, first=1)
            def _(j):
                other = (g + j) % pairs
                for which in range(2):
                    act(remote(slot(which, h, u), h, which, u,
                               lane_sem.at[h, which, j - 1, 1], (b, other * 2 + c)))
            for which in range(2):
                act(remote(slot(which, h, u), h, which, u,
                           pair_sem.at[h, which, 0, 1], (b, sibling)))

    def relay_2(h, act):
        @pl.when(has_2)
        def _():
            @functools.partial(each, pairs, looped, first=1)
            def _(j):
                other = (g + j) % pairs
                @pl.when(other < g)
                def _():
                    for which in range(2):
                        act(remote(slot(which, h, width + u), h, which, width + u,
                                   lane_sem.at[h, which, j - 1, 0], (b, other * 2 + c)))
            @pl.when(c == 1)
            def _():
                for which in range(2):
                    act(remote(slot(which, h, width + u), h, which, width + u,
                               pair_sem.at[h, which, 0, 0], (b, sibling)))

    def forward(h, j, recent, act):
        other = (g + j) % pairs
        index = (0 if recent else width) + other * 2 + c
        for which in range(2):
            act(remote(slot(which, h, index), h, which, index,
                       pair_sem.at[h, which, j, 1 if recent else 0], (b, sibling)))

    def both(h, j, act, wait):
        other = (g + j) % pairs
        lane = other * 2 + c
        @pl.when(has_1)
        def _():
            if wait:
                arrived(h, lane)
            forward(h, j, True, act)
        @pl.when((other < g) | has_2)
        def _():
            if wait:
                arrived(h, width + lane)
            forward(h, j, False, act)

    def start(copy):
        copy.start()

    def sent(copy):
        copy.wait_send()

    def first_stage(h):
        @pl.when(has_1)
        def _():
            arrived(h, u)
        relay_1(h, start)
        @pl.when(has_2)
        def _():
            arrived(h, width + u)
        relay_2(h, start)

    def second_stage(h):
        each(pairs, looped, lambda j: both(h, j, start, True), first=1)

    def third_stage(h):
        @pl.when(has_1)
        def _():
            arrived(h, sibling)
        @pl.when((c == 1) | has_2)
        def _():
            arrived(h, width + sibling)
        @functools.partial(each, pairs, looped, first=1)
        def _(j):
            other = (g + j) % pairs
            @pl.when(has_1)
            def _():
                arrived(h, other * 2 + 1 - c)
            @pl.when((other < g) | has_2)
            def _():
                arrived(h, width + other * 2 + 1 - c)

    query_copy = pltpu.make_async_copy(q_hbm, q_ref, local_sem.at[0, 0, 1])
    query_copy.start()

    def own_copy(h, act):
        for which in range(2):
            act(pltpu.make_async_copy(
                own(which, h), slot(which, h, 2 * width), local_sem.at[h, which, 0]))

    each(heads, looped, lambda h: own_copy(h, start))

    @pl.when(b < LOOK_BACK_BLOCKS)
    def _():
        @functools.partial(each, heads, looped)
        def _(h):
            for ref in win:
                ref[h, 0 : 2 * width * tokens, :] = jnp.zeros(
                    (2 * width * tokens, HEAD_WIDTH), ref.dtype)

    barrier = pltpu.get_barrier_semaphore()
    for distance in range(1, LOOK_BACK_BLOCKS + 1):
        @pl.when(b + distance < blocks)
        def _():
            pl.semaphore_signal(barrier, inc=1, device_id=(b + distance, u), device_id_type=MESH)
        @pl.when(b - distance >= 0)
        def _():
            pl.semaphore_signal(barrier, inc=1, device_id=(b - distance, u), device_id_type=MESH)
    for j in range(1, pairs):
        pl.semaphore_signal(
            barrier, inc=1, device_id=(b, ((g + j) % pairs) * 2 + c), device_id_type=MESH)
    pl.semaphore_signal(barrier, inc=1, device_id=(b, sibling), device_id_type=MESH)
    after = jnp.minimum(blocks - 1 - b, LOOK_BACK_BLOCKS)
    pl.semaphore_wait(barrier, jnp.minimum(b, LOOK_BACK_BLOCKS) + after + pairs)

    each(heads, looped, lambda h: shift_copies(h, start))
    lane_own(0, start)
    pair_own(0, start)

    starts = jnp.broadcast_to(start_ref[pl.ds(u, 1), :], (tokens, tokens)).T
    row = lax.broadcasted_iota(jnp.int32, (tokens, tokens), 0)
    column = lax.broadcasted_iota(jnp.int32, (tokens, tokens), 1)
    place = (b * width + u) * tokens + row

    def mask_tile(index, piece):
        key_place = piece * tokens + column
        seen = (key_place >= starts) & (key_place <= place)
        bias[:, pl.ds(pl.multiple_of(index * tokens, tokens), tokens)] = jnp.where(
            seen, 0.0, MASKED)

    each(width, looped, lambda i: mask_tile(i, (b - 1) * width + i))
    each(width, looped,
         lambda i: mask_tile(width + i, jnp.where(i < u, b, b - 2) * width + i))
    mask_tile(2 * width, b * width + u)

    def out_copy(h):
        columns = lanes(h, group)
        return pltpu.make_async_copy(o_ref.at[:, columns], o_hbm.at[:, columns], out_sem.at[h])

    factor = HEAD_WIDTH ** (-0.5) * LOG2_E

    def attend(h, step):
        base = h * group + step * batch
        queries = jnp.concatenate(
            [q_ref[:, lanes(base + i)] for i in range(batch)],
            axis=0)
        scores = lax.dot_general(
            queries, k_win[h], (((1,), (1,)), ((), ())), preferred_element_type=jnp.float32)
        scores = scores.reshape(batch, tokens, keys) + bias[...][None]
        top = jnp.max(scores, axis=-1, keepdims=True)
        exps = jnp.exp2((scores - top) * factor)
        totals = jnp.sum(exps, axis=-1, keepdims=True)
        blended = jnp.dot(
            exps.astype(jnp.bfloat16).reshape(batch * tokens, keys), v_win[h],
            preferred_element_type=jnp.float32)
        result = (blended.reshape(batch, tokens, HEAD_WIDTH) / totals).astype(o_ref.dtype)
        for i in range(batch):
            o_ref[:, lanes(base + i)] = result[i]

    def head_sends(h):
        @when(h < heads)
        def _():
            first_stage(h)
        @when(h + 1 < heads)
        def _():
            lane_own(h + 1, start)
            pair_own(h + 1, start)

    head_sends(0)
    head_sends(1)
    second_stage(0)
    query_copy.wait()
    each(heads, looped, lambda h: own_copy(h, lambda copy: copy.wait()))
    steps = group // batch

    @functools.partial(each, heads, looped)
    def _(h):
        third_stage(h)
        head_sends(h + 2)
        each(steps // 2, looped, lambda step: attend(h, step))
        @when(h + 1 < heads)
        def _():
            second_stage(h + 1)
        each(steps, looped, lambda step: attend(h, step), first=steps // 2)
        out_copy(h).start()

    @functools.partial(each, heads, looped)
    def _(h):
        shift_copies(h, sent)
        lane_own(h, sent)
        pair_own(h, sent)
        relay_1(h, sent)
        relay_2(h, sent)
        each(pairs, looped, lambda j: both(h, j, sent, False), first=1)
        out_copy(h).wait()


def local(query_projection, key_projection, value_projection, doc_start):
    blocks, width = lax.axis_size("blk"), lax.axis_size("uly")
    tokens, query_columns = query_projection.shape
    heads = key_projection.shape[1] // HEAD_WIDTH
    group = query_columns // HEAD_WIDTH // heads
    keys = (2 * width + 1) * tokens
    batch = group
    while batch > 1 and batch * tokens * keys > 640 * 1024:
        batch //= 2
    pairs = width // 2
    hbm = pl.BlockSpec(memory_space=pl.ANY)
    return pl.pallas_call(
        functools.partial(kernel, blocks, width, heads, group, batch),
        out_shape=jax.ShapeDtypeStruct(query_projection.shape, query_projection.dtype),
        in_specs=[hbm, hbm, hbm, pl.BlockSpec(memory_space=pltpu.VMEM)],
        out_specs=hbm,
        scratch_shapes=[
            pltpu.VMEM((tokens, query_columns), jnp.bfloat16),
            pltpu.VMEM((heads, keys, HEAD_WIDTH), jnp.bfloat16),
            pltpu.VMEM((heads, keys, HEAD_WIDTH), jnp.bfloat16),
            pltpu.VMEM((tokens, keys), jnp.float32),
            pltpu.VMEM((tokens, query_columns), jnp.bfloat16),
            pltpu.SemaphoreType.DMA((heads, 2, 2)),
            pltpu.SemaphoreType.DMA((heads,)),
            pltpu.SemaphoreType.DMA((heads, 2, LOOK_BACK_BLOCKS)),
            pltpu.SemaphoreType.DMA((heads, 2, max(1, pairs - 1), 2)),
            pltpu.SemaphoreType.DMA((heads, 2, pairs, 2)),
            pltpu.SemaphoreType.DMA((heads, 2, 2 * width)),
        ],
        compiler_params=pltpu.CompilerParams(
            collective_id=0, has_side_effects=True, vmem_limit_bytes=60 * 1024 * 1024),
    )(query_projection, key_projection, value_projection, doc_start.reshape(width, tokens))


def solution(mesh):
    placed = (P(("blk", "uly"), None), P(("blk", "uly"), None), P(("blk", "uly"), None), P("blk"))
    return jax.shard_map(
        local, mesh=mesh, in_specs=placed, out_specs=P(("blk", "uly"), None), check_vma=False
    )
```

```python
import functools

import jax
import jax.numpy as jnp
from jax import lax
from jax.experimental import pallas as pl
from jax.experimental.pallas import tpu as pltpu
from jax.sharding import PartitionSpec as P

HEAD_WIDTH = 128
LOOK_BACK_BLOCKS = 2
MASKED = -1e30
LOG2_E = 1.4426950408889634
MESH = pl.DeviceIdType.MESH


def each(count, looped, body, first=0):
    if looped:
        pl.loop(first, count)(body)
    else:
        for index in range(first, count):
            body(index)


def when(condition):
    if isinstance(condition, bool):
        return lambda body: body() if condition else None
    return pl.when(condition)


def kernel(
    blocks, width, heads, group, batch,
    q_hbm, k_hbm, v_hbm, start_ref, o_ref,
    q_ref, k_near, v_near, k_far, v_far, near_bias, far_bias, top_ref, sum_ref,
    query_sem, local_sem, shift_sem, lane_sem, pair_sem, near_sem, far_sem,
):
    tokens = q_hbm.shape[0]
    pairs = width // 2
    others = width - 1
    looped = pairs > 2
    b, u = lax.axis_index("blk"), lax.axis_index("uly")
    g, c = u // 2, u % 2
    sibling = g * 2 + (1 - c)
    has_1, has_2 = b >= 1, b >= 2
    hbm, nears, fars = (k_hbm, v_hbm), (k_near, v_near), (k_far, v_far)

    def rows(index):
        return pl.ds(pl.multiple_of(index * tokens, tokens), tokens)

    def lanes(index, count=1):
        span = count * HEAD_WIDTH
        return pl.ds(pl.multiple_of(index * span, span), span)

    def near(which, h, distance):
        return nears[which].at[h, rows(LOOK_BACK_BLOCKS - distance), :]

    def far_index(part, lane, owner):
        return part * others + (lane - owner + width) % width - 1

    def own(which, h):
        return hbm[which].at[:, lanes(h)]

    def shift(h, which, distance, device):
        return pltpu.make_async_remote_copy(
            src_ref=own(which, h),
            dst_ref=near(which, h, distance),
            send_sem=shift_sem.at[h, which, distance - 1],
            recv_sem=near_sem.at[h, which, distance - 1],
            device_id=device,
            device_id_type=MESH,
        )

    def remote(src, h, which, part, lane, send, target):
        index = far_index(part, lane, target)
        return pltpu.make_async_remote_copy(
            src_ref=src,
            dst_ref=fars[which].at[h, rows(index), :],
            send_sem=send,
            recv_sem=far_sem.at[h, which, index],
            device_id=(b, target),
            device_id_type=MESH,
        )

    def near_arrived(h, distance):
        for which in range(2):
            shift(h, which, distance, (b, sibling)).wait_recv()

    def far_ref(which, h, part, lane):
        return fars[which].at[h, rows(far_index(part, lane, u)), :]

    def far_arrived(h, part, lane):
        index = far_index(part, lane, u)
        for which in range(2):
            ref = far_ref(which, h, part, lane)
            pltpu.make_async_remote_copy(
                src_ref=ref,
                dst_ref=ref,
                send_sem=pair_sem.at[h, which, 0, 0],
                recv_sem=far_sem.at[h, which, index],
                device_id=(b, sibling),
                device_id_type=MESH,
            ).wait_recv()

    def shift_copies(h, act):
        for distance in range(1, LOOK_BACK_BLOCKS + 1):
            @pl.when(b + distance < blocks)
            def _():
                for which in range(2):
                    act(shift(h, which, distance, (b + distance, u)))

    def own_copies(h, act):
        @functools.partial(each, pairs, looped, first=1)
        def _(j):
            other = (g + j) % pairs
            @pl.when(other > g)
            def _():
                for which in range(2):
                    act(remote(own(which, h), h, which, 1, u,
                               lane_sem.at[h, which, j - 1, 0], other * 2 + c))
        @pl.when(c == 0)
        def _():
            for which in range(2):
                act(remote(own(which, h), h, which, 1, u, pair_sem.at[h, which, 0, 0], sibling))

    def relay_1(h, act):
        @pl.when(has_1)
        def _():
            @functools.partial(each, pairs, looped, first=1)
            def _(j):
                other = (g + j) % pairs
                for which in range(2):
                    act(remote(near(which, h, 1), h, which, 0, u,
                               lane_sem.at[h, which, j - 1, 1], other * 2 + c))
            for which in range(2):
                act(remote(near(which, h, 1), h, which, 0, u,
                           pair_sem.at[h, which, 0, 1], sibling))

    def relay_2(h, act):
        @pl.when(has_2)
        def _():
            @functools.partial(each, pairs, looped, first=1)
            def _(j):
                other = (g + j) % pairs
                @pl.when(other < g)
                def _():
                    for which in range(2):
                        act(remote(near(which, h, 2), h, which, 1, u,
                                   lane_sem.at[h, which, j - 1, 0], other * 2 + c))
            @pl.when(c == 1)
            def _():
                for which in range(2):
                    act(remote(near(which, h, 2), h, which, 1, u,
                               pair_sem.at[h, which, 0, 0], sibling))

    def forward(h, j, act, wait):
        other = (g + j) % pairs
        lane = other * 2 + c
        for part, there in ((1, (other < g) | has_2), (0, has_1)):
            @pl.when(there)
            def _():
                if wait:
                    far_arrived(h, part, lane)
                for which in range(2):
                    act(remote(far_ref(which, h, part, lane), h, which, part, lane,
                               pair_sem.at[h, which, j, 1 - part], sibling))

    def start(copy):
        copy.start()

    def sent(copy):
        copy.wait_send()

    def first_stage(h):
        @pl.when(has_1)
        def _():
            near_arrived(h, 1)
        relay_1(h, start)
        @pl.when(has_2)
        def _():
            near_arrived(h, 2)
        relay_2(h, start)

    def second_stage(h):
        each(pairs, looped, lambda j: forward(h, j, start, True), first=1)

    def third_stage(h):
        @pl.when(has_1)
        def _():
            far_arrived(h, 0, sibling)
        @pl.when((c == 1) | has_2)
        def _():
            far_arrived(h, 1, sibling)
        @functools.partial(each, pairs, looped, first=1)
        def _(j):
            other = (g + j) % pairs
            @pl.when(has_1)
            def _():
                far_arrived(h, 0, other * 2 + 1 - c)
            @pl.when((other < g) | has_2)
            def _():
                far_arrived(h, 1, other * 2 + 1 - c)

    @pl.when(b < LOOK_BACK_BLOCKS)
    def _():
        @functools.partial(each, heads, looped)
        def _(h):
            for ref in nears:
                size = LOOK_BACK_BLOCKS * tokens
                ref[h, 0:size, :] = jnp.zeros((size, HEAD_WIDTH), ref.dtype)
            for ref in fars:
                ref[h] = jnp.zeros(ref.shape[1:], ref.dtype)

    barrier = pltpu.get_barrier_semaphore()
    for distance in range(1, LOOK_BACK_BLOCKS + 1):
        @pl.when(b + distance < blocks)
        def _():
            pl.semaphore_signal(barrier, inc=1, device_id=(b + distance, u), device_id_type=MESH)
        @pl.when(b - distance >= 0)
        def _():
            pl.semaphore_signal(barrier, inc=1, device_id=(b - distance, u), device_id_type=MESH)
    for j in range(1, pairs):
        pl.semaphore_signal(
            barrier, inc=1, device_id=(b, ((g + j) % pairs) * 2 + c), device_id_type=MESH)
    pl.semaphore_signal(barrier, inc=1, device_id=(b, sibling), device_id_type=MESH)

    query_copy = pltpu.make_async_copy(q_hbm, q_ref, query_sem)
    query_copy.start()

    def fetch(h, act):
        for which in range(2):
            act(pltpu.make_async_copy(own(which, h), near(which, h, 0), local_sem.at[h, which]))

    each(heads, looped, lambda h: fetch(h, start))

    after = jnp.minimum(blocks - 1 - b, LOOK_BACK_BLOCKS)
    pl.semaphore_wait(barrier, jnp.minimum(b, LOOK_BACK_BLOCKS) + after + pairs)

    shift_copies(0, start)
    own_copies(0, start)
    each(heads, looped, lambda h: shift_copies(h, start), first=1)

    starts = jnp.broadcast_to(start_ref[pl.ds(u, 1), :], (tokens, tokens)).T
    row = lax.broadcasted_iota(jnp.int32, (tokens, tokens), 0)
    column = lax.broadcasted_iota(jnp.int32, (tokens, tokens), 1)
    place = (b * width + u) * tokens + row

    def mask_tile(ref, index, piece):
        key_place = piece * tokens + column
        seen = (key_place >= starts) & (key_place <= place)
        ref[:, rows(index)] = jnp.where(seen, 0.0, MASKED)

    for distance in range(LOOK_BACK_BLOCKS + 1):
        mask_tile(near_bias, LOOK_BACK_BLOCKS - distance, (b - distance) * width + u)

    @functools.partial(each, others, looped)
    def _(i):
        lane = (u + 1 + i) % width
        mask_tile(far_bias, i, (b - 1) * width + lane)
        mask_tile(far_bias, others + i, jnp.where(lane < u, b, b - 2) * width + lane)

    factor = HEAD_WIDTH ** (-0.5) * LOG2_E

    def scores_of(h, first, count, k_ref, bias):
        queries = jnp.concatenate(
            [q_ref[:, lanes(h * group + first + i)] for i in range(count)], axis=0)
        scores = lax.dot_general(
            queries, k_ref[h], (((1,), (1,)), ((), ())), preferred_element_type=jnp.float32)
        scores = scores.reshape(count, tokens, bias.shape[1]) + bias[...][None]
        scores = scores.reshape(count * tokens, bias.shape[1])
        return scores, jnp.max(scores, axis=-1, keepdims=True)

    def blend(scores, top, v_ref, h):
        weights = jnp.exp2((scores - top) * factor).astype(jnp.bfloat16)
        ones = jnp.ones((v_ref.shape[1], HEAD_WIDTH), jnp.bfloat16)
        values = jnp.concatenate([v_ref[h], ones], axis=1)
        return jnp.dot(weights, values, preferred_element_type=jnp.float32)

    def span(first, count):
        return pl.ds(pl.multiple_of(first * tokens, tokens), count * tokens)

    def attend_near(h):
        scores, top = scores_of(h, 0, group, k_near, near_bias)
        sum_ref[h] = blend(scores, top, v_near, h)
        top_ref[h] = jnp.broadcast_to(top, (group * tokens, HEAD_WIDTH))

    def attend_far(h, step):
        part = span(step * batch, batch)
        scores, top = scores_of(h, step * batch, batch, k_far, far_bias)
        before = top_ref[h, part, :]
        top = jnp.maximum(before[:, :1], top)
        fade = jnp.exp2((before - top) * factor)
        total = blend(scores, top, v_far, h)
        before = sum_ref[h, part, :]
        blended = before[:, :HEAD_WIDTH] * fade + total[:, :HEAD_WIDTH]
        totals = before[:, HEAD_WIDTH:] * fade + total[:, HEAD_WIDTH:]
        result = (blended / totals).astype(o_ref.dtype)
        for i in range(batch):
            o_ref[:, lanes(h * group + step * batch + i)] = result[i * tokens : (i + 1) * tokens]

    query_copy.wait()
    each(heads, looped, lambda h: fetch(h, lambda copy: copy.wait()))

    @functools.partial(each, heads, looped)
    def _(h):
        first_stage(h)
        @when(h + 1 < heads)
        def _():
            own_copies(h + 1, start)
        @when(h == heads - 1)
        def _():
            second_stage(0)
        attend_near(h)

    steps = group // batch

    @functools.partial(each, heads, looped)
    def _(h):
        third_stage(h)
        each(steps // 2, looped, lambda step: attend_far(h, step))
        @when(h + 1 < heads)
        def _():
            second_stage(h + 1)
        each(steps, looped, lambda step: attend_far(h, step), first=steps // 2)

    @functools.partial(each, heads, looped)
    def _(h):
        shift_copies(h, sent)
        own_copies(h, sent)
        relay_1(h, sent)
        relay_2(h, sent)
        each(pairs, looped, lambda j: forward(h, j, sent, False), first=1)


def local(query_projection, key_projection, value_projection, doc_start):
    blocks, width = lax.axis_size("blk"), lax.axis_size("uly")
    tokens, query_columns = query_projection.shape
    heads = key_projection.shape[1] // HEAD_WIDTH
    group = query_columns // HEAD_WIDTH // heads
    near_keys = (LOOK_BACK_BLOCKS + 1) * tokens
    far_keys = LOOK_BACK_BLOCKS * (width - 1) * tokens
    batch = group
    while batch > 1 and batch * tokens * far_keys > 640 * 1024:
        batch //= 2
    pairs = width // 2
    hbm = pl.BlockSpec(memory_space=pl.ANY)
    vmem = pl.BlockSpec(memory_space=pltpu.VMEM)
    return pl.pallas_call(
        functools.partial(kernel, blocks, width, heads, group, batch),
        out_shape=pltpu.VMEM(query_projection.shape, query_projection.dtype),
        in_specs=[hbm, hbm, hbm, vmem],
        out_specs=vmem,
        scratch_shapes=[
            pltpu.VMEM((tokens, query_columns), jnp.bfloat16),
            pltpu.VMEM((heads, near_keys, HEAD_WIDTH), jnp.bfloat16),
            pltpu.VMEM((heads, near_keys, HEAD_WIDTH), jnp.bfloat16),
            pltpu.VMEM((heads, far_keys, HEAD_WIDTH), jnp.bfloat16),
            pltpu.VMEM((heads, far_keys, HEAD_WIDTH), jnp.bfloat16),
            pltpu.VMEM((tokens, near_keys), jnp.float32),
            pltpu.VMEM((tokens, far_keys), jnp.float32),
            pltpu.VMEM((heads, group * tokens, HEAD_WIDTH), jnp.float32),
            pltpu.VMEM((heads, group * tokens, 2 * HEAD_WIDTH), jnp.float32),
            pltpu.SemaphoreType.DMA,
            pltpu.SemaphoreType.DMA((heads, 2)),
            pltpu.SemaphoreType.DMA((heads, 2, LOOK_BACK_BLOCKS)),
            pltpu.SemaphoreType.DMA((heads, 2, max(1, pairs - 1), 2)),
            pltpu.SemaphoreType.DMA((heads, 2, pairs, 2)),
            pltpu.SemaphoreType.DMA((heads, 2, LOOK_BACK_BLOCKS)),
            pltpu.SemaphoreType.DMA((heads, 2, 2 * (width - 1))),
        ],
        compiler_params=pltpu.CompilerParams(
            collective_id=0, has_side_effects=True, vmem_limit_bytes=56 * 1024 * 1024),
    )(query_projection, key_projection, value_projection, doc_start.reshape(width, tokens))


def solution(mesh):
    placed = (P(("blk", "uly"), None), P(("blk", "uly"), None), P(("blk", "uly"), None), P("blk"))
    return jax.shard_map(
        local, mesh=mesh, in_specs=placed, out_specs=P(("blk", "uly"), None), check_vma=False
    )
```

```python
import functools

import jax
import jax.numpy as jnp
from jax import lax
from jax.experimental import pallas as pl
from jax.experimental.pallas import tpu as pltpu
from jax.sharding import PartitionSpec as P

HEAD_WIDTH = 128
LOOK_BACK_BLOCKS = 2
MASKED = -1e30
LOG2_E = 1.4426950408889634
MESH = pl.DeviceIdType.MESH


def each(count, looped, body, first=0):
    if looped:
        pl.loop(first, count)(body)
    else:
        for index in range(first, count):
            body(index)


def when(condition):
    if isinstance(condition, bool):
        return lambda body: body() if condition else None
    return pl.when(condition)


def kernel(
    blocks, width, heads, group, batch,
    q_hbm, k_hbm, v_hbm, start_ref, o_ref,
    q_ref, k_near, v_near, k_far, v_far, near_bias, far_bias, top_ref, sum_ref,
    query_sem, local_sem, shift_sem, lane_sem, pair_sem, near_sem, far_sem,
):
    tokens = q_hbm.shape[0]
    pairs = width // 2
    others = width - 1
    looped = pairs > 2
    b, u = lax.axis_index("blk"), lax.axis_index("uly")
    g, c = u // 2, u % 2
    sibling = g * 2 + (1 - c)
    has_1, has_2 = b >= 1, b >= 2
    hbm, nears, fars = (k_hbm, v_hbm), (k_near, v_near), (k_far, v_far)

    def rows(index):
        return pl.ds(pl.multiple_of(index * tokens, tokens), tokens)

    def lanes(index, count=1):
        span = count * HEAD_WIDTH
        return pl.ds(pl.multiple_of(index * span, span), span)

    def near(which, h, distance):
        return nears[which].at[h, rows(LOOK_BACK_BLOCKS - distance), :]

    def far_index(part, lane, owner):
        return part * others + (lane - owner + width) % width - 1

    def own(which, h):
        return hbm[which].at[:, lanes(h)]

    def shift(h, which, distance, device):
        return pltpu.make_async_remote_copy(
            src_ref=own(which, h),
            dst_ref=near(which, h, distance),
            send_sem=shift_sem.at[h, which, distance - 1],
            recv_sem=near_sem.at[h, which, distance - 1],
            device_id=device,
            device_id_type=MESH,
        )

    def remote(src, h, which, part, lane, send, target):
        index = far_index(part, lane, target)
        return pltpu.make_async_remote_copy(
            src_ref=src,
            dst_ref=fars[which].at[h, rows(index), :],
            send_sem=send,
            recv_sem=far_sem.at[h, which, index],
            device_id=(b, target),
            device_id_type=MESH,
        )

    def near_arrived(h, distance):
        for which in range(2):
            shift(h, which, distance, (b, sibling)).wait_recv()

    def far_ref(which, h, part, lane):
        return fars[which].at[h, rows(far_index(part, lane, u)), :]

    def far_arrived(h, part, lane):
        index = far_index(part, lane, u)
        for which in range(2):
            ref = far_ref(which, h, part, lane)
            pltpu.make_async_remote_copy(
                src_ref=ref,
                dst_ref=ref,
                send_sem=pair_sem.at[h, which, 0, 0],
                recv_sem=far_sem.at[h, which, index],
                device_id=(b, sibling),
                device_id_type=MESH,
            ).wait_recv()

    def shift_copies(h, act):
        for distance in range(1, LOOK_BACK_BLOCKS + 1):
            @pl.when(b + distance < blocks)
            def _():
                for which in range(2):
                    act(shift(h, which, distance, (b + distance, u)))

    def own_copies(h, act):
        @functools.partial(each, pairs, looped, first=1)
        def _(j):
            other = (g + j) % pairs
            @pl.when(other > g)
            def _():
                for which in range(2):
                    act(remote(own(which, h), h, which, 1, u,
                               lane_sem.at[h, which, j - 1, 0], other * 2 + c))
        @pl.when(c == 0)
        def _():
            for which in range(2):
                act(remote(own(which, h), h, which, 1, u, pair_sem.at[h, which, 0, 0], sibling))

    def relay_1(h, act):
        @pl.when(has_1)
        def _():
            @functools.partial(each, pairs, looped, first=1)
            def _(j):
                other = (g + j) % pairs
                for which in range(2):
                    act(remote(near(which, h, 1), h, which, 0, u,
                               lane_sem.at[h, which, j - 1, 1], other * 2 + c))
            for which in range(2):
                act(remote(near(which, h, 1), h, which, 0, u,
                           pair_sem.at[h, which, 0, 1], sibling))

    def relay_2(h, act):
        @pl.when(has_2)
        def _():
            @functools.partial(each, pairs, looped, first=1)
            def _(j):
                other = (g + j) % pairs
                @pl.when(other < g)
                def _():
                    for which in range(2):
                        act(remote(near(which, h, 2), h, which, 1, u,
                                   lane_sem.at[h, which, j - 1, 0], other * 2 + c))
            @pl.when(c == 1)
            def _():
                for which in range(2):
                    act(remote(near(which, h, 2), h, which, 1, u,
                               pair_sem.at[h, which, 0, 0], sibling))

    def forward(h, j, act, wait):
        other = (g + j) % pairs
        lane = other * 2 + c
        for part, there in ((1, (other < g) | has_2), (0, has_1)):
            @pl.when(there)
            def _():
                if wait:
                    far_arrived(h, part, lane)
                for which in range(2):
                    act(remote(far_ref(which, h, part, lane), h, which, part, lane,
                               pair_sem.at[h, which, j, 1 - part], sibling))

    def start(copy):
        copy.start()

    def sent(copy):
        copy.wait_send()

    def first_stage(h):
        @pl.when(has_1)
        def _():
            near_arrived(h, 1)
        relay_1(h, start)
        @pl.when(has_2)
        def _():
            near_arrived(h, 2)
        relay_2(h, start)

    def second_stage(h):
        each(pairs, looped, lambda j: forward(h, j, start, True), first=1)

    def third_stage(h):
        @pl.when(has_1)
        def _():
            far_arrived(h, 0, sibling)
        @pl.when((c == 1) | has_2)
        def _():
            far_arrived(h, 1, sibling)
        @functools.partial(each, pairs, looped, first=1)
        def _(j):
            other = (g + j) % pairs
            @pl.when(has_1)
            def _():
                far_arrived(h, 0, other * 2 + 1 - c)
            @pl.when((other < g) | has_2)
            def _():
                far_arrived(h, 1, other * 2 + 1 - c)

    @pl.when(b < LOOK_BACK_BLOCKS)
    def _():
        @functools.partial(each, heads, looped)
        def _(h):
            for ref in nears:
                size = LOOK_BACK_BLOCKS * tokens
                ref[h, 0:size, :] = jnp.zeros((size, HEAD_WIDTH), ref.dtype)
            for ref in fars:
                ref[h] = jnp.zeros(ref.shape[1:], ref.dtype)

    barrier = pltpu.get_barrier_semaphore()
    for distance in range(1, LOOK_BACK_BLOCKS + 1):
        @pl.when(b + distance < blocks)
        def _():
            pl.semaphore_signal(barrier, inc=1, device_id=(b + distance, u), device_id_type=MESH)
        @pl.when(b - distance >= 0)
        def _():
            pl.semaphore_signal(barrier, inc=1, device_id=(b - distance, u), device_id_type=MESH)
    for j in range(1, pairs):
        pl.semaphore_signal(
            barrier, inc=1, device_id=(b, ((g + j) % pairs) * 2 + c), device_id_type=MESH)
    pl.semaphore_signal(barrier, inc=1, device_id=(b, sibling), device_id_type=MESH)

    query_copy = pltpu.make_async_copy(q_hbm, q_ref, query_sem)
    query_copy.start()

    def fetch(h, act):
        for which in range(2):
            act(pltpu.make_async_copy(own(which, h), near(which, h, 0), local_sem.at[h, which]))

    each(heads, looped, lambda h: fetch(h, start))

    after = jnp.minimum(blocks - 1 - b, LOOK_BACK_BLOCKS)
    pl.semaphore_wait(barrier, jnp.minimum(b, LOOK_BACK_BLOCKS) + after + pairs)

    shift_copies(0, start)
    own_copies(0, start)
    each(heads, looped, lambda h: shift_copies(h, start), first=1)

    starts = jnp.broadcast_to(start_ref[pl.ds(u, 1), :], (tokens, tokens)).T
    row = lax.broadcasted_iota(jnp.int32, (tokens, tokens), 0)
    column = lax.broadcasted_iota(jnp.int32, (tokens, tokens), 1)
    place = (b * width + u) * tokens + row

    def mask_tile(ref, index, piece):
        key_place = piece * tokens + column
        seen = (key_place >= starts) & (key_place <= place)
        ref[:, rows(index)] = jnp.where(seen, 0.0, MASKED)

    for distance in range(LOOK_BACK_BLOCKS + 1):
        mask_tile(near_bias, LOOK_BACK_BLOCKS - distance, (b - distance) * width + u)

    @functools.partial(each, others, looped)
    def _(i):
        lane = (u + 1 + i) % width
        mask_tile(far_bias, i, (b - 1) * width + lane)
        mask_tile(far_bias, others + i, jnp.where(lane < u, b, b - 2) * width + lane)

    factor = HEAD_WIDTH ** (-0.5) * LOG2_E

    def scores_of(h, first, count, k_ref, bias):
        queries = jnp.concatenate(
            [q_ref[:, lanes(h * group + first + i)] for i in range(count)], axis=0)
        scores = lax.dot_general(
            queries, k_ref[h], (((1,), (1,)), ((), ())), preferred_element_type=jnp.float32)
        scores = scores.reshape(count, tokens, bias.shape[1]) + bias[...][None]
        scores = scores.reshape(count * tokens, bias.shape[1])
        return scores, jnp.max(scores, axis=-1, keepdims=True)

    def blend(scores, top, v_ref, h):
        weights = jnp.exp2((scores - top) * factor).astype(jnp.bfloat16)
        ones = jnp.ones((v_ref.shape[1], HEAD_WIDTH), jnp.bfloat16)
        values = jnp.concatenate([v_ref[h], ones], axis=1)
        return jnp.dot(weights, values, preferred_element_type=jnp.float32)

    def span(first, count):
        return pl.ds(pl.multiple_of(first * tokens, tokens), count * tokens)

    def attend_near(h):
        scores, top = scores_of(h, 0, group, k_near, near_bias)
        sum_ref[h] = blend(scores, top, v_near, h)
        top_ref[h] = jnp.broadcast_to(top, (group * tokens, HEAD_WIDTH))

    def attend_far(h, step):
        part = span(step * batch, batch)
        scores, top = scores_of(h, step * batch, batch, k_far, far_bias)
        before = top_ref[h, part, :]
        top = jnp.maximum(before[:, :1], top)
        fade = jnp.exp2((before - top) * factor)
        total = blend(scores, top, v_far, h)
        before = sum_ref[h, part, :]
        blended = before[:, :HEAD_WIDTH] * fade + total[:, :HEAD_WIDTH]
        totals = before[:, HEAD_WIDTH:] * fade + total[:, HEAD_WIDTH:]
        result = (blended / totals).astype(o_ref.dtype)
        for i in range(batch):
            o_ref[:, lanes(h * group + step * batch + i)] = result[i * tokens : (i + 1) * tokens]

    query_copy.wait()
    each(heads, looped, lambda h: fetch(h, lambda copy: copy.wait()))

    def take(h):
        @when(h < heads)
        def _():
            first_stage(h)
        @when(h + 1 < heads)
        def _():
            own_copies(h + 1, start)

    take(0)
    attend_near(0)
    take(1)
    second_stage(0)
    attend_near(1)
    steps = group // batch

    @functools.partial(each, heads, looped)
    def _(h):
        third_stage(h)
        each(steps // 2, looped, lambda step: attend_far(h, step))
        take(h + 2)
        @when(h + 1 < heads)
        def _():
            second_stage(h + 1)
        each(steps, looped, lambda step: attend_far(h, step), first=steps // 2)
        @when(h + 2 < heads)
        def _():
            attend_near(h + 2)

    @functools.partial(each, heads, looped)
    def _(h):
        shift_copies(h, sent)
        own_copies(h, sent)
        relay_1(h, sent)
        relay_2(h, sent)
        each(pairs, looped, lambda j: forward(h, j, sent, False), first=1)


def local(query_projection, key_projection, value_projection, doc_start):
    blocks, width = lax.axis_size("blk"), lax.axis_size("uly")
    tokens, query_columns = query_projection.shape
    heads = key_projection.shape[1] // HEAD_WIDTH
    group = query_columns // HEAD_WIDTH // heads
    near_keys = (LOOK_BACK_BLOCKS + 1) * tokens
    far_keys = LOOK_BACK_BLOCKS * (width - 1) * tokens
    batch = group
    while batch > 1 and batch * tokens * far_keys > 640 * 1024:
        batch //= 2
    pairs = width // 2
    hbm = pl.BlockSpec(memory_space=pl.ANY)
    vmem = pl.BlockSpec(memory_space=pltpu.VMEM)
    return pl.pallas_call(
        functools.partial(kernel, blocks, width, heads, group, batch),
        out_shape=pltpu.VMEM(query_projection.shape, query_projection.dtype),
        in_specs=[hbm, hbm, hbm, vmem],
        out_specs=vmem,
        scratch_shapes=[
            pltpu.VMEM((tokens, query_columns), jnp.bfloat16),
            pltpu.VMEM((heads, near_keys, HEAD_WIDTH), jnp.bfloat16),
            pltpu.VMEM((heads, near_keys, HEAD_WIDTH), jnp.bfloat16),
            pltpu.VMEM((heads, far_keys, HEAD_WIDTH), jnp.bfloat16),
            pltpu.VMEM((heads, far_keys, HEAD_WIDTH), jnp.bfloat16),
            pltpu.VMEM((tokens, near_keys), jnp.float32),
            pltpu.VMEM((tokens, far_keys), jnp.float32),
            pltpu.VMEM((heads, group * tokens, HEAD_WIDTH), jnp.float32),
            pltpu.VMEM((heads, group * tokens, 2 * HEAD_WIDTH), jnp.float32),
            pltpu.SemaphoreType.DMA,
            pltpu.SemaphoreType.DMA((heads, 2)),
            pltpu.SemaphoreType.DMA((heads, 2, LOOK_BACK_BLOCKS)),
            pltpu.SemaphoreType.DMA((heads, 2, max(1, pairs - 1), 2)),
            pltpu.SemaphoreType.DMA((heads, 2, pairs, 2)),
            pltpu.SemaphoreType.DMA((heads, 2, LOOK_BACK_BLOCKS)),
            pltpu.SemaphoreType.DMA((heads, 2, 2 * (width - 1))),
        ],
        compiler_params=pltpu.CompilerParams(
            collective_id=0, has_side_effects=True, vmem_limit_bytes=56 * 1024 * 1024),
    )(query_projection, key_projection, value_projection, doc_start.reshape(width, tokens))


def solution(mesh):
    placed = (P(("blk", "uly"), None), P(("blk", "uly"), None), P(("blk", "uly"), None), P("blk"))
    return jax.shard_map(
        local, mesh=mesh, in_specs=placed, out_specs=P(("blk", "uly"), None), check_vma=False
    )
```
